32 devices in a mesh: seq: 8 (over y, x, core), hx: 4 (over z).
Axes of the slice: x: 2, y: 2, z: 4, core: 2. Of those that a mesh axis runs over, the one named last changes fastest.
Arguments:
- hidden_in: bfloat16 [256, 4, 2048], P('seq'), may hold values from -6 to 6
- q_span: bfloat16 [256, 4, 2048], P('seq', None, 'hx'), may hold values from -4.6 to 4.6
- k_span: bfloat16 [256, 4, 2048], P('seq', None, 'hx'), may hold values from -4.6 to 4.6
- v_span: bfloat16 [256, 4, 2048], P('seq', None, 'hx'), may hold values from -4 to 4
- k_cache: bfloat16 [4, 4096, 2048], P(None, 'seq', 'hx'), may hold values from -4 to 4
- v_cache: bfloat16 [4, 4096, 2048], P(None, 'seq', 'hx'), may hold values from -4 to 4
- lengths: int32 [4], replicated, may hold values from 512 to 4096, as said below
- block_map: int32 [4, 32], P(None, 'seq'), may hold values 0 or 1
- w_out: bfloat16 [2048, 2048], P('hx'), may hold values from -0.125 to 0.125
- norm_gain: bfloat16 [2048], replicated, may hold values from 0.5 to 1.5
- routes: int32 [256, 4, 4], P('seq'), may hold values from 0 to 7, all different within a row; in each aligned block of 128 rows (0 to 127, 128 to 255, ..., all dimensions but the last counted through in order) at most 128 rows name the same one
- route_weights: float32 [256, 4, 4], P('seq'), may hold values from 0.05 to 0.5
- w_gate_up: bfloat16 [8, 2048, 2, 1408], P('seq', None, None, 'hx'), may hold values from -0.125 to 0.125
- w_down: bfloat16 [8, 1408, 2048], P('seq', 'hx'), may hold values from -0.15625 to 0.15625
- shared_gate_up: bfloat16 [2048, 2, 2816], P(None, None, 'hx'), may hold values from -0.125 to 0.125
- shared_down: bfloat16 [2816, 2048], P('hx'), may hold values from -0.109375 to 0.109375
- shared_gate_vec: bfloat16 [2048], replicated, may hold values from -0.125 to 0.125
- next_gain: bfloat16 [2048], replicated, may hold values from 0.5 to 1.5
- w_next: bfloat16 [2048, 3, 2048], P(None, None, 'hx'), may hold values from -0.125 to 0.125
Outputs:
- hidden_out: bfloat16 [256, 4, 2048], P('seq', None, 'hx')
- next_qkv: bfloat16 [256, 4, 3, 2048], P('seq', None, None, 'hx')
The draws below stay inside these ranges and needn't reach their ends.
Inputs may be any that keep to these rules, and one draw needn't show every extreme that they name: `lengths`: one request has exactly 4096 cached tokens and another exactly 512. `routes`: each token names 4 different experts; in the rows of one device (128 tokens in the order of the first two dimensions) no expert is named more than 128 times, a bound that some block reaches.
All inputs are finite; a program needn't handle non-finite values. No bound on the sum of `block_map` on one device may be relied on, other than what follows from the above.
Results may differ from the reference program's by a relative error of at most 0.015.
Values may be sent and summed in bfloat16 or wider, within the bound.
A program may use at most 128 MiB of HBM per device.

```python
import math
import jax
import jax.numpy as jnp
import numpy as np
from jax import lax

D = 2048
H = 16
HD = 128
FFE = 1408
SHARED = 2816
TOP = 4
R = 4
BLK = 128
EXPERTS = 8
SPAN = 256
LMAX = 4096
NBLK = 32
TOK_DEV = 128
CAP = 128
N_SEQ = 8


def draw_q_span(key, part):
    array_shape = (SPAN, R, H * HD)
    drawn = jnp.clip(jax.random.normal(jax.random.fold_in(key, 1), array_shape, jnp.float32), -4.0, 4.0)
    return drawn.astype(jnp.bfloat16)


def draw_k_span(key, part):
    array_shape = (SPAN, R, H * HD)
    drawn = jnp.clip(jax.random.normal(jax.random.fold_in(key, 5), array_shape, jnp.float32), -4.0, 4.0)
    return drawn.astype(jnp.bfloat16)


def draw_lengths(key, part):
    drawn = jax.random.randint(jax.random.fold_in(key, 6), (R,), LMAX // 8, LMAX + 1)
    order = jax.random.permutation(jax.random.fold_in(key, 7), R)
    drawn = drawn.at[order[0]].set(LMAX).at[order[1]].set(LMAX // 8)
    return drawn.astype(jnp.int32)


def set_ends(values, rng, least, largest):
    longest = values.shape.index(max(values.shape))
    spots = []
    for shift in (0, 1):
        where = [jax.random.randint(jax.random.fold_in(rng, axis), (), 0, length) for axis, length in enumerate(values.shape)]
        where[longest] = (where[longest] + shift) % values.shape[longest]
        spots.append(tuple(where))
    return values.at[spots[0]].set(least).at[spots[1]].set(largest)


def block_levels(key, shape, split, smallest, top_value):
    factor_of, own = 1.0, jax.random.fold_in(key, 6)
    for dim, shards_of in split:
        steps = jnp.exp(jax.random.uniform(jax.random.fold_in(own, dim), (shards_of,), jnp.float32, smallest / len(split), top_value / len(split)))
        factor_of = factor_of * jnp.repeat(steps, shape[dim] // shards_of).reshape([-1 if axis == dim else 1 for axis in range(len(shape))])
    return factor_of


def deal_out(own_key, own, number, rows, count, top, bound, slope):
    sequence = jax.random.permutation(own_key, count)
    packed, usual = load_shares(count, rows * top, bound, slope, True), load_shares(count, rows * top, bound, slope, False)
    places = jnp.arange(count)

    def named(tallies, offset_by):
        used = int((tallies > 0).sum())
        fixed = max(1, used // 4)
        shifted = fixed + (places - fixed + offset_by * (used - fixed)) % max(1, count - fixed)
        return jnp.zeros((count,), jnp.int32).at[sequence[jnp.where(places < fixed, places, shifted)]].set(jnp.asarray(tallies, jnp.int32))

    tallies = jnp.where(number % 4 == 0, named(packed, number // 4), named(usual, number - number // 4 - 1))
    mixed = jax.random.permutation(jax.random.fold_in(own, 3), count)
    giver, receiver = mixed[0:count // 2 * 2:2], mixed[1:count // 2 * 2:2]
    room = jnp.minimum(tallies[giver] - 1, bound - tallies[receiver]) // 2
    room = jnp.where((giver == sequence[0]) | (receiver == sequence[0]) | (tallies[receiver] == 0), 0, jnp.maximum(room, 0))
    shifted = jax.random.randint(jax.random.fold_in(own, 4), (count // 2,), 0, 1 << 20) % (room + 1)
    tallies = tallies.at[giver].add(-shifted).at[receiver].add(shifted)
    items = jnp.searchsorted(jnp.cumsum(tallies), jnp.arange(rows * top), side="right").astype(jnp.int32)
    listing = items.reshape(top, rows).T
    listing = listing[jax.random.permutation(jax.random.fold_in(own, 1), rows)]
    offset_by = jax.random.randint(jax.random.fold_in(own, 2), (rows, 1), 0, top)
    return jnp.take_along_axis(listing, (jnp.arange(top)[None, :] + offset_by) % top, axis=1)


def load_shares(count, total, bound, slope, full):
    loads = [(1 << 20) // math.isqrt(standing ** slope) + 1 for standing in range(1, count + 1)]
    largest = bound if full else min(bound, max(-(-total // count), total * loads[0] // sum(loads)))
    least = 1 if total - largest >= count - 1 else 0
    given, rest = [largest] + [least] * (count - 1), total - largest - least * (count - 1)
    while rest > 0:
        free = [i for i in range(1, count) if given[i] < largest] or [i for i in range(1, count) if given[i] < bound]
        pool, budget = sum([loads[i] for i in free]), rest
        for i in free:
            extra = min(bound - given[i], max(1, budget * loads[i] // pool), rest)
            given[i] = given[i] + extra
            rest = rest - extra
    return np.array(given)


def bell_draw(own_key, shape, deviation, reach, cuts=(), kind=jnp.bfloat16):
    entries = deviation * jax.random.normal(own_key, shape, jnp.float32)
    if cuts:
        entries = entries * block_levels(own_key, shape, cuts, -0.22, 0.18)
    return jnp.clip(entries, -reach, reach).astype(kind)


def setup_inputs(seed: int = 0) -> dict:
    key_of = jax.random.split(jax.random.key(seed), 20)
    hidden_in = bell_draw(key_of[0], (SPAN, R, D), 1.0, 6.0, ((0, 8),))
    q_span = draw_q_span(jax.random.fold_in(key_of[19], 71), 0)
    k_span = draw_k_span(jax.random.fold_in(key_of[19], 71), 0)
    v_span = bell_draw(key_of[3], (SPAN, R, H * HD), 1.0, 4.0, ((0, 8), (2, 4)))
    k_cache = bell_draw(key_of[4], (R, LMAX, H * HD), 1.0, 4.0, ((1, 8), (2, 4)))
    v_cache = bell_draw(key_of[5], (R, LMAX, H * HD), 1.0, 4.0, ((1, 8), (2, 4)))
    lengths = draw_lengths(jax.random.fold_in(key_of[19], 71), 0)
    block_map = set_ends((jax.random.randint(key_of[7], (R, NBLK), 0, 4) < 3).astype(jnp.int32), jax.random.fold_in(key_of[7], 1), 0, 1)
    w_out = bell_draw(key_of[8], (H * HD, D), (H * HD) ** -0.5, 0.125, ((0, 4),))
    norm_gain = jnp.clip(1.0 + 0.1 * jax.random.normal(key_of[9], (D,), jnp.float32), 0.5, 1.5).astype(jnp.bfloat16)
    routes_keys = jax.random.split(jax.random.fold_in(key_of[10], 1), SPAN * R // TOK_DEV)
    routes_turns = jax.random.permutation(jax.random.fold_in(key_of[10], 3), SPAN * R // TOK_DEV)
    routes = jax.vmap(lambda own, number: deal_out(jax.random.fold_in(key_of[10], 2), own, number, TOK_DEV, EXPERTS, TOP, CAP, 2))(routes_keys, routes_turns).reshape((SPAN, R, TOP))
    route_weights = jnp.clip(0.05 + 0.45 * jax.random.uniform(key_of[11], (SPAN, R, TOP), jnp.float32) ** block_levels(key_of[11], (SPAN, R, TOP), ((0, 8),), -0.2, 0.2), 0.05, 0.5)
    w_gate_up = bell_draw(key_of[12], (EXPERTS, D, 2, FFE), D ** -0.5, 0.125, ((0, 8), (3, 4)))
    w_down = bell_draw(key_of[13], (EXPERTS, FFE, D), FFE ** -0.5, 0.15625, ((0, 8), (1, 4)))
    shared_gate_up = bell_draw(key_of[14], (D, 2, SHARED), D ** -0.5, 0.125, ((2, 4),))
    shared_down = bell_draw(key_of[15], (SHARED, D), SHARED ** -0.5, 0.109375, ((0, 4),))
    shared_gate_vec = bell_draw(key_of[16], (D,), D ** -0.5, 0.125)
    next_gain = jnp.clip(1.0 + 0.1 * jax.random.normal(key_of[17], (D,), jnp.float32), 0.5, 1.5).astype(jnp.bfloat16)
    w_next = bell_draw(key_of[18], (D, 3, H * HD), D ** -0.5, 0.125, ((2, 4),))
    return dict(hidden_in=hidden_in, q_span=q_span, k_span=k_span, v_span=v_span, k_cache=k_cache, v_cache=v_cache, lengths=lengths, block_map=block_map, w_out=w_out, norm_gain=norm_gain, routes=routes, route_weights=route_weights, w_gate_up=w_gate_up, w_down=w_down, shared_gate_up=shared_gate_up, shared_down=shared_down, shared_gate_vec=shared_gate_vec, next_gain=next_gain, w_next=w_next)


NEG_FILL = -1e+30
EPSILON = 1e-06

def normalize(token_rows, gain_vec):
    return token_rows * lax.rsqrt(lax.optimization_barrier(jnp.mean(token_rows * token_rows, -1, keepdims=True)) + EPSILON) * gain_vec.astype(jnp.float32)

def expert_block(token_rows, gate_up, down_proj):
    unit_count = gate_up.shape[2]
    gate_up_out = jnp.dot(token_rows, gate_up.reshape(gate_up.shape[0], 2 * unit_count), preferred_element_type=jnp.float32)
    hidden = (jax.nn.silu(gate_up_out[:, :unit_count]) * gate_up_out[:, unit_count:]).astype(jnp.bfloat16)
    return jnp.dot(hidden, down_proj, preferred_element_type=jnp.float32)

def expert_apply(operands):
    return expert_block(operands[0], operands[1], operands[2])

def reference(hidden_in, q_span, k_span, v_span, k_cache, v_cache, lengths, block_map, w_out, norm_gain, routes, route_weights, w_gate_up, w_down, shared_gate_up, shared_down, shared_gate_vec, next_gain, w_next):
    token_count = SPAN * R
    head_width = H * HD
    query_pos = jnp.arange(SPAN, dtype=jnp.int32)
    slot_pos = jnp.arange(LMAX, dtype=jnp.int32)
    block_live = jnp.repeat(block_map, BLK, axis=1)
    causal = query_pos[None, :] <= query_pos[:, None]
    attended_list = []
    for request in range(R):
        cache_live = (slot_pos < lengths[request]) & (block_live[request] == 1)
        visible = jnp.concatenate([jnp.broadcast_to(cache_live[None, :], (SPAN, LMAX)), causal], 1)
        queries = q_span[:, request].reshape(SPAN, H, HD).transpose(1, 0, 2)
        key_rows = jnp.concatenate([k_cache[request], k_span[:, request]], 0).reshape(LMAX + SPAN, H, HD).transpose(1, 0, 2)
        value_rows = jnp.concatenate([v_cache[request], v_span[:, request]], 0).reshape(LMAX + SPAN, H, HD).transpose(1, 0, 2)

        def one_head(operands, visible=visible):
            query_h, key_h, value_h = operands
            scores = jnp.dot(query_h, key_h.T, preferred_element_type=jnp.float32) / math.sqrt(HD)
            scores = jnp.where(visible, scores, NEG_FILL)
            row_peak = lax.optimization_barrier(jnp.max(scores, 1, keepdims=True))
            weights = jnp.where(visible, jnp.exp(scores - row_peak), 0.0)
            mixed_out = jnp.dot(weights.astype(jnp.bfloat16), value_h, preferred_element_type=jnp.float32)
            return (mixed_out / lax.optimization_barrier(jnp.sum(weights, 1, keepdims=True))).astype(jnp.bfloat16)
        per_head = lax.map(one_head, (queries, key_rows, value_rows))
        attended_list.append(per_head.transpose(1, 0, 2).reshape(SPAN, head_width))
    attended = jnp.stack(attended_list, 1).reshape(token_count, head_width)
    first = (hidden_in.reshape(token_count, D).astype(jnp.float32) + jnp.dot(attended, w_out, preferred_element_type=jnp.float32)).astype(jnp.bfloat16)
    normed_one = normalize(first.astype(jnp.float32), norm_gain).astype(jnp.bfloat16)
    flat_routes = routes.reshape(token_count * TOP).astype(jnp.int32)
    onehot = (flat_routes[:, None] == jnp.arange(EXPERTS, dtype=jnp.int32)[None, :]).astype(jnp.int32)
    blocked = onehot.reshape(N_SEQ, TOK_DEV * TOP, EXPERTS)
    running = jnp.cumsum(blocked, 1).astype(jnp.int32)
    slot_rank = lax.optimization_barrier(jnp.sum((running - blocked) * blocked, 2)).astype(jnp.int32).reshape(token_count * TOP)
    entry_ids = jnp.arange(token_count * TOP, dtype=jnp.int32)
    column = (entry_ids // (TOK_DEV * TOP) * CAP + slot_rank).astype(jnp.int32)
    source_rows = normed_one[entry_ids // TOP]
    buffer = jnp.zeros((EXPERTS, N_SEQ * CAP, D), jnp.bfloat16).at[flat_routes, column].set(source_rows)
    expert_out = lax.map(expert_apply, (buffer, w_gate_up, w_down))
    picked = expert_out[flat_routes, column]
    routed = lax.optimization_barrier(jnp.sum(picked.reshape(token_count, TOP, D) * route_weights.reshape(token_count, TOP, 1).astype(jnp.float32), 1))
    shared_lift = jax.nn.sigmoid(jnp.dot(normed_one, shared_gate_vec, preferred_element_type=jnp.float32))
    shared = shared_lift[:, None] * expert_block(normed_one, shared_gate_up, shared_down)
    whole = (first.astype(jnp.float32) + routed + shared).astype(jnp.bfloat16)
    normed_two = normalize(whole.astype(jnp.float32), next_gain).astype(jnp.bfloat16)
    following = jnp.dot(normed_two, w_next.reshape(D, 3 * head_width), preferred_element_type=jnp.float32).astype(jnp.bfloat16)
    return (whole.reshape(SPAN, R, D), following.reshape(SPAN, R, 3, head_width))
```

```python
import math

import jax
import jax.numpy as jnp
from jax import lax
from jax.experimental import pallas as pl
from jax.experimental.pallas import tpu as pltpu
from jax.sharding import PartitionSpec as P

HD = 128
BLK = 128


NEG_FILL = -1e30
EPSILON = 1e-06


def normalize(token_rows, gain_vec):
    return (
        token_rows
        * lax.rsqrt(jnp.mean(token_rows * token_rows, -1, keepdims=True) + EPSILON)
        * gain_vec.astype(jnp.float32)
    )


def expert_block(token_rows, gate_up, down_proj):
    unit_count = gate_up.shape[2]
    gate_up_out = jnp.dot(
        token_rows,
        gate_up.reshape(gate_up.shape[0], 2 * unit_count),
        preferred_element_type=jnp.float32,
    )
    hidden = (jax.nn.silu(gate_up_out[:, :unit_count]) * gate_up_out[:, unit_count:]).astype(
        jnp.bfloat16
    )
    return jnp.dot(hidden, down_proj, preferred_element_type=jnp.float32)


FLOOR = -1e4
MESH = pl.DeviceIdType.MESH
VMEM_SPEC = pl.BlockSpec(memory_space=pltpu.VMEM)
VMEM_BYTES = 48 * 1024 * 1024


def attend_kernel(heads, q_ref, k_ref, v_ref, ks_ref, vs_ref, live_ref, causal_ref, out_ref, stat):
    unit = pl.program_id(0) * heads + pl.program_id(1)
    units = pl.num_programs(0) * pl.num_programs(1)
    contract = (((1,), (1,)), ((), ()))
    scale = 1.0 / math.sqrt(HD)
    queries = q_ref[...]
    cached = (
        lax.dot_general(queries, k_ref[0], contract, preferred_element_type=jnp.float32) * scale
        + live_ref[0]
    )
    fresh = (
        lax.dot_general(queries, ks_ref[...], contract, preferred_element_type=jnp.float32) * scale
        + causal_ref[...]
    )
    peak = jnp.maximum(
        jnp.max(cached, 1, keepdims=True), jnp.max(fresh, 1, keepdims=True)
    )
    peak = jnp.maximum(peak, FLOOR).astype(jnp.bfloat16).astype(jnp.float32)
    cached = jnp.exp(cached - peak)
    fresh = jnp.exp(fresh - peak)
    total = jnp.sum(cached, 1, keepdims=True) + jnp.sum(fresh, 1, keepdims=True)
    mixed = jnp.dot(
        cached.astype(jnp.bfloat16), v_ref[0], preferred_element_type=jnp.float32
    ) + jnp.dot(fresh.astype(jnp.bfloat16), vs_ref[...], preferred_element_type=jnp.float32)
    out_ref[:, pl.ds(pl.multiple_of(unit * HD, HD), HD)] = mixed.astype(jnp.bfloat16)
    high = total.astype(jnp.bfloat16).astype(jnp.float32)
    lane = lax.broadcasted_iota(jnp.int32, stat.shape, 1)

    @pl.when(unit == 0)
    def _():
        stat[...] = jnp.zeros_like(stat)

    held = stat[...]
    held = jnp.where(lane == unit, peak, held)
    held = jnp.where(lane == unit + units, high, held)
    held = jnp.where(lane == unit + 2 * units, total - high, held)
    stat[...] = held

    @pl.when(unit == units - 1)
    def _():
        out_ref[:, pl.ds(pl.multiple_of(units * HD, HD), HD)] = held.astype(jnp.bfloat16)


def attend(queries, k_cache, v_cache, k_new, v_new, live, causal):
    requests, cache_dev, width_q = k_cache.shape
    heads = width_q // HD
    span_all = queries.shape[0]
    span_dev = k_new.shape[0]
    width_out = (requests * heads + 1) * HD
    return pl.pallas_call(
        lambda *refs: attend_kernel(heads, *refs),
        grid=(requests, heads),
        in_specs=[
            pl.BlockSpec((span_all, HD), lambda r, h: (0, r * heads + h)),
            pl.BlockSpec((1, cache_dev, HD), lambda r, h: (r, 0, h)),
            pl.BlockSpec((1, cache_dev, HD), lambda r, h: (r, 0, h)),
            pl.BlockSpec((span_dev, HD), lambda r, h: (0, r * heads + h)),
            pl.BlockSpec((span_dev, HD), lambda r, h: (0, r * heads + h)),
            pl.BlockSpec((1, 1, cache_dev), lambda r, h: (r, 0, 0)),
            pl.BlockSpec((span_all, span_dev), lambda r, h: (0, 0)),
        ],
        out_specs=pl.BlockSpec((span_all, width_out), lambda r, h: (0, 0)),
        out_shape=jax.ShapeDtypeStruct((span_all, width_out), jnp.bfloat16),
        scratch_shapes=[pltpu.VMEM((span_all, HD), jnp.float32)],
        compiler_params=pltpu.CompilerParams(vmem_limit_bytes=VMEM_BYTES),
        name="attend",
    )(queries, k_cache, v_cache, k_new, v_new, live, causal)


def merge_kernel(units, got_ref, out_ref):
    stat = got_ref[:, :, units * HD :].astype(jnp.float32)
    peak = stat[:, :, :units]
    total = stat[:, :, units : 2 * units] + stat[:, :, 2 * units : 3 * units]
    factor = jnp.exp(peak - jnp.max(peak, 0, keepdims=True))
    share = factor / jnp.sum(total * factor, 0, keepdims=True)
    for unit in range(units):
        part = got_ref[:, :, unit * HD : (unit + 1) * HD].astype(jnp.float32)
        out_ref[:, unit * HD : (unit + 1) * HD] = jnp.sum(
            part * share[:, :, unit : unit + 1], 0
        ).astype(jnp.bfloat16)


def merge(got, units):
    return pl.pallas_call(
        lambda *refs: merge_kernel(units, *refs),
        in_specs=[VMEM_SPEC],
        out_specs=VMEM_SPEC,
        out_shape=jax.ShapeDtypeStruct((got.shape[1], units * HD), jnp.bfloat16),
        compiler_params=pltpu.CompilerParams(vmem_limit_bytes=VMEM_BYTES),
        name="merge",
    )(got)


def send(src, dst, send_sem, recv_sem, axis, peer):
    return pltpu.make_async_remote_copy(
        src_ref=src,
        dst_ref=dst,
        send_sem=send_sem,
        recv_sem=recv_sem,
        device_id={axis: peer},
        device_id_type=MESH,
    )


def greet(axis, peers):
    barrier = pltpu.get_barrier_semaphore()
    for peer in peers:
        pl.semaphore_signal(barrier, inc=1, device_id={axis: peer}, device_id_type=MESH)
    pl.semaphore_wait(barrier, len(peers))


def sum_hx_kernel(n, x_ref, res_ref, out_ref, slots, sends, recvs):
    me = lax.axis_index("hx")
    rows = x_ref.shape[0] // n
    peers = [lax.rem(me + step, n) for step in range(1, n)]

    def part(ref, index):
        return ref.at[pl.ds(pl.multiple_of(index * rows, rows), rows)]

    greet("hx", peers)
    copies = []
    for step in range(1, n):
        copies.append(
            send(
                part(x_ref, peers[step - 1]), slots.at[step - 1],
                sends.at[0, step - 1], recvs.at[0, step - 1], "hx", peers[step - 1],
            )
        )
        copies[-1].start()
    mine = pl.ds(pl.multiple_of(me * rows, rows), rows)
    total = x_ref[mine, :].astype(jnp.float32)
    for step in range(1, n):
        copies[step - 1].wait_recv()
        total = total + slots[step - 1].astype(jnp.float32)
    out_ref[mine, :] = (res_ref[mine, :].astype(jnp.float32) + total).astype(jnp.bfloat16)
    for step in range(1, n):
        copies.append(
            send(
                part(out_ref, me), part(out_ref, me),
                sends.at[1, step - 1], recvs.at[1, step - 1], "hx", peers[step - 1],
            )
        )
        copies[-1].start()
    for step in range(1, n):
        source = part(out_ref, lax.rem(me + n - step, n))
        send(
            source, source, sends.at[1, step - 1], recvs.at[1, step - 1], "hx", peers[step - 1]
        ).wait_recv()
    for copy in copies:
        copy.wait_send()


def sum_hx(x, residual, number):
    n = lax.axis_size("hx")
    return pl.pallas_call(
        lambda *refs: sum_hx_kernel(n, *refs),
        in_specs=[VMEM_SPEC] * 2,
        out_specs=VMEM_SPEC,
        out_shape=jax.ShapeDtypeStruct(x.shape, jnp.bfloat16),
        scratch_shapes=[
            pltpu.VMEM((n - 1, x.shape[0] // n, x.shape[1]), jnp.bfloat16),
            pltpu.SemaphoreType.DMA((2, n - 1)),
            pltpu.SemaphoreType.DMA((2, n - 1)),
        ],
        compiler_params=pltpu.CompilerParams(
            collective_id=number, has_side_effects=True, vmem_limit_bytes=VMEM_BYTES
        ),
        name="sum_hx",
    )(x, residual)


def bit_orders(n):
    bits = list(range(n.bit_length() - 1))
    other = list(bits)
    if len(bits) > 1:
        other[-1], other[-2] = other[-2], other[-1]
    return bits, other


def flipped(me, mask):
    where = me
    for bit in range(mask.bit_length()):
        if mask >> bit & 1:
            where = where + (1 - 2 * lax.rem(me // (1 << bit), 2)) * (1 << bit)
    return where


def spread_seq_kernel(n, x_ref, out_ref, sends, recvs, own_sem):
    me = lax.axis_index("seq")
    half = x_ref.shape[1] // 2
    orders = [order[::-1] for order in bit_orders(n)]
    spots = [flipped(me, mask) for mask in range(n)]

    def part(mask, side):
        return out_ref.at[spots[mask], :, pl.ds(side * half, half)]

    own = pltpu.make_async_copy(x_ref, out_ref.at[me], own_sem)
    own.start()
    greet("seq", [spots[1 << bit] for bit in orders[0]])
    copies = []
    held = [[0], [0]]
    for level in range(len(orders[0])):
        for index in range(len(held[0])):
            for side in range(2):
                bit = 1 << orders[side][level]
                mask = held[side][index]
                source = x_ref.at[:, pl.ds(side * half, half)] if mask == 0 else part(mask, side)
                copies.append(
                    send(
                        source, part(mask, side), sends.at[side, mask | bit],
                        recvs.at[side, mask | bit], "seq", spots[bit],
                    )
                )
                copies[-1].start()
        for side in range(2):
            bit = 1 << orders[side][level]
            new = [mask | bit for mask in held[side]]
            for mask in new:
                send(
                    part(mask, side), part(mask, side), sends.at[side, mask],
                    recvs.at[side, mask], "seq", spots[bit],
                ).wait_recv()
            held[side] = held[side] + new
    for copy in copies:
        copy.wait_send()
    own.wait()


def spread_seq(x, number):
    n = lax.axis_size("seq")
    return pl.pallas_call(
        lambda *refs: spread_seq_kernel(n, *refs),
        in_specs=[VMEM_SPEC],
        out_specs=VMEM_SPEC,
        out_shape=jax.ShapeDtypeStruct((n,) + x.shape, jnp.bfloat16),
        scratch_shapes=[
            pltpu.SemaphoreType.DMA((2, n)),
            pltpu.SemaphoreType.DMA((2, n)),
            pltpu.SemaphoreType.DMA,
        ],
        compiler_params=pltpu.CompilerParams(
            collective_id=number, has_side_effects=True, vmem_limit_bytes=VMEM_BYTES
        ),
        name="spread_seq",
    )(x)


def collect_seq_kernel(n, x_ref, add_ref, out_ref, slots, held, sends, recvs):
    me = lax.axis_index("seq")
    half = x_ref.shape[2] // 2
    orders = bit_orders(n)
    spots = [flipped(me, mask) for mask in range(n)]
    greet("seq", [spots[1 << bit] for bit in orders[0]])
    masks = [list(range(n)), list(range(n))]
    copies = []
    for level in range(len(orders[0])):
        waits = []
        for side in range(2):
            columns = pl.ds(side * half, half)
            bit = 1 << orders[side][level]
            for mask in masks[side]:
                if mask & bit:
                    source = x_ref.at[spots[mask], :, columns] if level == 0 else held.at[mask, :, columns]
                    copies.append(
                        send(
                            source, slots.at[mask, :, columns], sends.at[side, mask],
                            recvs.at[side, mask], "seq", spots[bit],
                        )
                    )
                    copies[-1].start()
                    waits.append((copies[-1], side, mask, bit))
            masks[side] = [mask for mask in masks[side] if not mask & bit]
        last = level == len(orders[0]) - 1
        for copy, side, mask, bit in waits:
            columns = slice(side * half, (side + 1) * half)
            keep = mask - bit
            copy.wait_recv()
            mine = x_ref[spots[keep], :, columns] if level == 0 else held[keep, :, columns]
            total = mine.astype(jnp.float32) + slots[mask, :, columns].astype(jnp.float32)
            if last:
                out_ref[:, columns] = (total + add_ref[:, columns]).astype(jnp.bfloat16)
            else:
                held[keep, :, columns] = total.astype(jnp.bfloat16)
    for copy in copies:
        copy.wait_send()


def collect_seq(x, add, number):
    n = x.shape[0]
    return pl.pallas_call(
        lambda *refs: collect_seq_kernel(n, *refs),
        in_specs=[VMEM_SPEC] * 2,
        out_specs=VMEM_SPEC,
        out_shape=jax.ShapeDtypeStruct(x.shape[1:], jnp.bfloat16),
        scratch_shapes=[
            pltpu.VMEM(x.shape, jnp.bfloat16),
            pltpu.VMEM(x.shape, jnp.bfloat16),
            pltpu.SemaphoreType.DMA((2, n)),
            pltpu.SemaphoreType.DMA((2, n)),
        ],
        compiler_params=pltpu.CompilerParams(
            collective_id=number, has_side_effects=True, vmem_limit_bytes=56 * 1024 * 1024
        ),
        name="collect_seq",
    )(x, add)


def local(
    hidden_in,
    q_span,
    k_span,
    v_span,
    k_cache,
    v_cache,
    lengths,
    block_map,
    w_out,
    norm_gain,
    routes,
    route_weights,
    w_gate_up,
    w_down,
    shared_gate_up,
    shared_down,
    shared_gate_vec,
    next_gain,
    w_next,
):
    span_dev, requests, width_q = q_span.shape
    heads_local = width_q // HD
    cache_dev = k_cache.shape[1]
    model_width = hidden_in.shape[2]
    seq_count = lax.axis_size("seq")
    hx_count = lax.axis_size("hx")
    seq_pos = lax.axis_index("seq")
    hx_pos = lax.axis_index("hx")
    span_all = span_dev * seq_count
    token_count = span_dev * requests
    width_part = model_width // hx_count
    units = requests * heads_local
    queries = lax.all_gather(q_span.reshape(span_dev, units * HD), "seq", axis=0, tiled=True)
    query_pos = jnp.arange(span_all, dtype=jnp.int32)
    new_pos = seq_pos * span_dev + jnp.arange(span_dev, dtype=jnp.int32)
    slot_pos = seq_pos * cache_dev + jnp.arange(cache_dev, dtype=jnp.int32)
    block_live = jnp.repeat(block_map, BLK, axis=1)
    live = (slot_pos[None, :] < lengths[:, None]) & (block_live == 1)
    live = jnp.where(live, 0.0, NEG_FILL).astype(jnp.float32)[:, None, :]
    causal = jnp.where(new_pos[None, :] <= query_pos[:, None], 0.0, NEG_FILL).astype(jnp.float32)
    mixed = attend(
        queries,
        k_cache,
        v_cache,
        k_span.reshape(span_dev, units * HD),
        v_span.reshape(span_dev, units * HD),
        live,
        causal,
    )
    got = lax.all_to_all(
        mixed.reshape(seq_count, span_dev, mixed.shape[1]),
        "seq",
        split_axis=0,
        concat_axis=0,
        tiled=True,
    )
    attended = merge(got, units).reshape(token_count, width_q)
    head_terms = jnp.dot(attended, w_out, preferred_element_type=jnp.float32).astype(jnp.bfloat16)
    first = sum_hx(head_terms, hidden_in.reshape(token_count, model_width), 1)
    normed_one = normalize(first.astype(jnp.float32), norm_gain).astype(jnp.bfloat16)
    exp_dev = w_gate_up.shape[0]
    experts_all = exp_dev * seq_count
    top_count = routes.shape[2]
    onehot = (
        routes.reshape(token_count, top_count, 1)
        == jnp.arange(experts_all, dtype=jnp.int32)[None, None, :]
    )
    spread = jnp.sum(
        jnp.where(onehot, route_weights.reshape(token_count, top_count, 1), 0.0), 1
    )
    own_weights = lax.all_to_all(
        spread.T.reshape(seq_count, exp_dev, token_count),
        "seq",
        split_axis=0,
        concat_axis=0,
        tiled=True,
    )
    shared_lift = jax.nn.sigmoid(
        jnp.dot(normed_one, shared_gate_vec, preferred_element_type=jnp.float32)
    )
    shared = shared_lift[:, None] * expert_block(normed_one, shared_gate_up, shared_down)
    token_rows = spread_seq(normed_one, 2).reshape(seq_count * token_count, model_width)
    terms = sum(
        own_weights[:, index].reshape(seq_count * token_count, 1)
        * expert_block(token_rows, w_gate_up[index], w_down[index])
        for index in range(exp_dev)
    )
    combined = collect_seq(
        terms.astype(jnp.bfloat16).reshape(seq_count, token_count, model_width), shared, 3
    )
    whole = sum_hx(combined, first, 4)
    result = lax.dynamic_slice_in_dim(whole, hx_pos * width_part, width_part, 1)
    normed = normalize(whole.astype(jnp.float32), next_gain).astype(jnp.bfloat16)
    following = jnp.einsum(
        "tm,mcw->tcw", normed, w_next, preferred_element_type=jnp.float32
    ).astype(jnp.bfloat16)
    return (
        result.reshape(span_dev, requests, width_part),
        following.reshape(span_dev, requests, 3, width_q),
    )


def solution(mesh):
    placed = (
        P("seq", None, None),
        P("seq", None, "hx"),
        P("seq", None, "hx"),
        P("seq", None, "hx"),
        P(None, "seq", "hx"),
        P(None, "seq", "hx"),
        P(),
        P(None, "seq"),
        P("hx", None),
        P(),
        P("seq", None, None),
        P("seq", None, None),
        P("seq", None, None, "hx"),
        P("seq", "hx", None),
        P(None, None, "hx"),
        P("hx", None),
        P(),
        P(),
        P(None, None, "hx"),
    )
    return jax.shard_map(
        local,
        mesh=mesh,
        in_specs=placed,
        out_specs=(P("seq", None, "hx"), P("seq", None, None, "hx")),
        check_vma=False,
    )
```
